256 devices in a mesh: row: 32 (over x_hi, z, core), col: 8 (over x_lo, y).
Axes of the slice: x: 4 (x_hi: 2, x_lo: 2; x = x_hi * 2 + x_lo), y: 4, z: 8, core: 2. Of those that a mesh axis runs over, the one named last changes fastest.
Arguments:
- amplitudes: float32 [1024, 64, 1200], P('col', 'row'), may hold values from -6 to 6
- integrals: float32 [64, 1200, 8, 1200], P('row', None, 'col'), may hold values from -0.09375 to 0.09375
- pair_energy: float32 [1024], P(('row', 'col')), may hold values from -4 to -1
- block_energy: float32 [8], replicated, may hold values from 0.2 to 3
- virtual_energy: float32 [1200], replicated, may hold values from 0.2 to 3
Outputs:
- new_amplitudes: float32 [1024, 8, 1200], P(('row', 'col'))
The draws below stay inside these ranges and needn't reach their ends.
All inputs are finite; a program needn't handle non-finite values.
Results may differ from the reference program's by a relative error of at most 0.00027.
Values sent between devices are 32-bit elements; how exact they have to be, the bound alone decides.
A program may use at most 128 MiB of HBM per device.

```python
import jax
import jax.numpy as jnp
from jax import lax

NV = 1200
PAIRS = 1024
CB = 64
AB = 8


def shard_levels(own_key, dims, pieces, low, largest):
    factor_of, own = 1.0, jax.random.fold_in(own_key, 6)
    for dim, blocks in pieces:
        steps = jnp.exp(jax.random.uniform(jax.random.fold_in(own, dim), (blocks,), jnp.float32, low / len(pieces), largest / len(pieces)))
        factor_of = factor_of * jnp.repeat(steps, dims[dim] // blocks).reshape([-1 if axis == dim else 1 for axis in range(len(dims))])
    return factor_of


def gaussian(key, shape, width, limit, shards=(), dtype=jnp.bfloat16):
    gain = shard_levels(key, shape, shards, -0.22, 0.18) if shards else 1.0
    entries = jax.random.normal(key, shape, jnp.float32) * width * gain
    return jnp.minimum(jnp.maximum(entries, -limit), limit).astype(dtype)


def setup_inputs(seed: int = 0) -> dict:
    seeds = jax.random.split(jax.random.key(seed), 6)
    return {
        "amplitudes": gaussian(seeds[0], (PAIRS, CB, NV), 1.0, 6.0, ((0, 8), (1, 32)), jnp.float32),
        "integrals": gaussian(seeds[1], (CB, NV, AB, NV), (CB * NV // 16) ** -0.5, 0.09375, ((0, 32), (2, 8)), jnp.float32),
        "pair_energy": jnp.clip(-4.0 + 3.0 * jax.random.uniform(seeds[2], (PAIRS,), jnp.float32) ** shard_levels(seeds[2], (PAIRS,), ((0, 256),), -0.2, 0.2), -4.0, -1.0),
        "block_energy": jnp.clip(jax.random.uniform(seeds[3], (AB,), jnp.float32, 0.2, 3.0), 0.2, 3.0),
        "virtual_energy": jnp.clip(jax.random.uniform(seeds[4], (NV,), jnp.float32, 0.2, 3.0), 0.2, 3.0),
    }


def reference(amplitudes, integrals, pair_energy, block_energy, virtual_energy):
    flattened = amplitudes.reshape(PAIRS, CB * NV)
    matrix = integrals.reshape(CB * NV, AB * NV)
    ladder = jnp.dot(flattened, matrix, precision=lax.Precision.HIGHEST, preferred_element_type=jnp.float32)
    ladder = ladder.reshape(PAIRS, AB, NV)
    denominator = pair_energy[:, None, None] - block_energy[None, :, None] - virtual_energy[None, None, :]
    return ladder / denominator
```

```python
import functools

import jax
import jax.numpy as jnp
from jax import lax
from jax.experimental import pallas as pl
from jax.experimental.pallas import tpu as pltpu
from jax.sharding import PartitionSpec as P

MESH = pl.DeviceIdType.MESH

OWN, LEFT, RIGHT, ACROSS, ACROSS_LEFT, ACROSS_RIGHT, FAR, ACROSS_FAR = range(8)
Y_SIZE, Z_SIZE = 4, 8
PAIRS = 128
WIDTH = 1200
PADDED = 1280
HALF = PADDED // 2
DEPTH = 2400
TILE = 480
TILES = DEPTH // TILE
TILE_PAD = 512
STAGE = 240
STAGES = DEPTH // STAGE
SLOTS = 4
SPLIT = 3 * TILE
FIRST = (0, SPLIT)
SECOND = (SPLIT, DEPTH - SPLIT)
BLOCK = PAIRS // Z_SIZE
PART = BLOCK // 2
QUAD = 4
COLUMN = 256


def halves(rows):
    start, size = rows
    return (start, size // 2), (start + size // 2, size // 2)


def kernel(
    amp_ref,
    int_ref,
    pair_ref,
    block_ref,
    virt_ref,
    out_ref,
    gathered,
    stage,
    b_high,
    b_low,
    lhs,
    partial,
    core_in,
    summed,
    z_in,
    z_sum,
    x_in,
    quads,
    final,
    own_sem,
    stage_sem,
    up_send,
    up_recv,
    down_send,
    down_recv,
    over_send,
    over_recv,
    core_send,
    core_recv,
    z_send,
    z_recv,
    x_send,
    x_recv,
    final_send,
    final_recv,
):
    row = lax.axis_index("row")
    col = lax.axis_index("col")
    x_hi, z, core = row // 16, (row // 2) % Z_SIZE, row % 2
    x_lo, y = col // Y_SIZE, col % Y_SIZE

    up = {"row": row, "col": x_lo * Y_SIZE + (y + 1) % Y_SIZE}
    down = {"row": row, "col": x_lo * Y_SIZE + (y + 3) % Y_SIZE}
    over = {"row": row, "col": (1 - x_lo) * Y_SIZE + y}
    partner = {"row": row + 1 - 2 * core, "col": col}
    opposite = {"row": row + 16 - 32 * x_hi, "col": col}

    def at_z(step):
        return {"row": x_hi * 16 + ((z + step) % Z_SIZE) * 2 + core, "col": col}

    def load(index):
        slot = index % SLOTS
        source = int_ref.at[index // 5, pl.ds((index % 5) * STAGE, STAGE), 0]
        return pltpu.make_async_copy(source, stage.at[slot], stage_sem.at[slot])

    own_copy = pltpu.make_async_copy(amp_ref, gathered.at[OWN], own_sem)
    for index in range(SLOTS):
        load(index).start()

    barrier = pltpu.get_barrier_semaphore()

    def greet(device):
        pl.semaphore_signal(barrier, inc=1, device_id=device, device_id_type=MESH)

    for device in (up, down, over, partner, opposite):
        greet(device)
    for step in range(1, Z_SIZE):
        greet(at_z(step))
    source_z = 2 * (row % 4) + col // 4
    source_row = ((col % 4) // 2) * 16 + source_z * 2
    for other_col in range(8):
        for other_core in range(2):
            greet({"row": source_row + other_core, "col": other_col})
    own_copy.start()
    pl.semaphore_wait(barrier, 5 + 7 + 16)

    sends = []

    def send(source, target, send_sem, recv_sem, device):
        copy = pltpu.make_async_remote_copy(
            src_ref=source,
            dst_ref=target,
            send_sem=send_sem,
            recv_sem=recv_sem,
            device_id=device,
            device_id_type=MESH,
        )
        copy.start()
        return copy

    def landed(ref, sem):
        pltpu.make_async_copy(ref, ref, sem).wait()

    counts = {"up": 0, "down": 0, "over": 0}
    lanes = {
        "up": (up, up_send, up_recv),
        "down": (down, down_send, down_recv),
        "over": (over, over_send, over_recv),
    }
    arrivals = {}

    def forward(lane, source, target, rows):
        device, send_sem, recv_sem = lanes[lane]
        index = counts[lane]
        counts[lane] = index + 1
        start, size = rows
        if source == OWN:
            source_ref = amp_ref.at[pl.ds(start, size)]
        else:
            source_ref = gathered.at[source, pl.ds(start, size)]
        target_ref = gathered.at[target, pl.ds(start, size)]
        sends.append(send(source_ref, target_ref, send_sem.at[index], recv_sem.at[index], device))
        arrivals[(lane, target, rows)] = (target_ref, recv_sem.at[index])

    def arrived(lane, target, rows):
        landed(*arrivals.pop((lane, target, rows)))

    low_half, high_half = range(2)
    second_halves, first_halves = halves(SECOND), halves(FIRST)

    forward("up", OWN, LEFT, SECOND)
    forward("down", OWN, RIGHT, SECOND)
    forward("over", OWN, ACROSS, FIRST)
    forward("up", OWN, LEFT, FIRST)
    forward("down", OWN, RIGHT, FIRST)
    forward("over", OWN, ACROSS, SECOND)

    for tile in range(TILES):
        zeros = jnp.zeros((TILE_PAD - TILE, PADDED), jnp.bfloat16)
        b_high[pl.ds(tile * TILE_PAD + TILE, TILE_PAD - TILE), :] = zeros
        b_low[pl.ds(tile * TILE_PAD + TILE, TILE_PAD - TILE), :] = zeros

    def prepare(index, carry):
        load(index).wait()
        value = stage[index % SLOTS]
        high = value.astype(jnp.bfloat16)
        low = (value - high.astype(jnp.float32)).astype(jnp.bfloat16)
        start = pl.multiple_of((index // 2) * TILE_PAD + (index % 2) * STAGE, 16)
        b_high[pl.ds(start, STAGE), pl.ds(0, WIDTH)] = high
        b_low[pl.ds(start, STAGE), pl.ds(0, WIDTH)] = low

        @pl.when(index + SLOTS < STAGES)
        def _():
            load(index + SLOTS).start()

        return carry

    def split(slot, place, places, first, last):
        def body(tile, carry):
            value = gathered[slot, pl.ds(pl.multiple_of(tile * TILE, 8), TILE), :]
            value = jnp.concatenate([value, jnp.zeros((TILE_PAD - TILE, PAIRS), jnp.float32)], axis=0).T
            high = value.astype(jnp.bfloat16)
            low = (value - high.astype(jnp.float32)).astype(jnp.bfloat16)
            lanes_of = pl.ds(pl.multiple_of(tile * TILE_PAD, TILE_PAD), TILE_PAD)
            lhs[pl.ds(place * PAIRS, PAIRS), lanes_of] = high
            lhs[pl.ds((places + place) * PAIRS, PAIRS), lanes_of] = low
            return carry

        lax.fori_loop(first, last, body, 0)

    def multiply(slots, first, last, add):
        places = len(slots)
        rows = places * PAIRS
        for place, slot in enumerate(slots):
            split(slot, place, places, first, last)
        depth = pl.ds(first * TILE_PAD, (last - first) * TILE_PAD)

        def body(step, carry):
            columns = pl.ds(pl.multiple_of(step * COLUMN, COLUMN), COLUMN)
            both = jnp.dot(lhs[pl.ds(0, 2 * rows), depth], b_high[depth, columns], preferred_element_type=jnp.float32)
            rest = jnp.dot(lhs[pl.ds(0, rows), depth], b_low[depth, columns], preferred_element_type=jnp.float32)
            total = both[:rows] + (both[rows:] + rest)
            for place, slot in enumerate(slots):
                piece = total[place * PAIRS : (place + 1) * PAIRS]
                if add:
                    piece = piece + partial[slot, :, columns]
                partial[slot, :, columns] = piece
            return carry

        lax.fori_loop(0, PADDED // COLUMN, body, 0)

    kept = pl.ds(pl.multiple_of(core * HALF, 128), HALF)
    given = pl.ds(pl.multiple_of((1 - core) * HALF, 128), HALF)

    def to_core(slot):
        sends.append(
            send(partial.at[slot, :, given], core_in.at[slot], core_send.at[slot], core_recv.at[slot], partner)
        )

    def to_z(slot):
        landed(core_in.at[slot], core_recv.at[slot])
        summed[slot] = partial[slot, :, kept] + core_in[slot]
        for step in range(1, Z_SIZE):
            start = pl.multiple_of(((z + step) % Z_SIZE) * BLOCK, BLOCK)
            send(
                summed.at[slot, pl.ds(start, BLOCK)],
                z_in.at[slot, step - 1],
                z_send.at[slot],
                z_recv.at[slot],
                at_z(step),
            )

    def to_x(slot):
        landed(z_in.at[slot], z_recv.at[slot])
        total = summed[slot, pl.ds(pl.multiple_of(z * BLOCK, BLOCK), BLOCK), :]
        for step in range(Z_SIZE - 1):
            total = total + z_in[slot, step]
        z_sum[slot] = total
        start = pl.multiple_of((1 - x_hi) * PART, PART)
        sends.append(
            send(z_sum.at[slot, pl.ds(start, PART)], x_in.at[slot], x_send.at[slot], x_recv.at[slot], opposite)
        )

    def chunk_col(slot):
        shift = {OWN: 0, LEFT: 3, RIGHT: 1, ACROSS: 0, ACROSS_LEFT: 3, ACROSS_RIGHT: 1, FAR: 2, ACROSS_FAR: 2}[slot]
        side = x_lo if slot in (OWN, LEFT, RIGHT, FAR) else 1 - x_lo
        return side * Y_SIZE + (y + shift) % Y_SIZE

    owners = []

    def to_owner(slot):
        landed(x_in.at[slot], x_recv.at[slot])
        total = z_sum[slot, pl.ds(pl.multiple_of(x_hi * PART, PART), PART), :] + x_in[slot]
        owner_row = 4 * chunk_col(slot) + z // 2
        for quad in range(2):
            quads[slot, quad] = total[quad * QUAD : (quad + 1) * QUAD]
            owner_col = 4 * (z % 2) + 2 * x_hi + quad
            here = jnp.logical_and(owner_row == row, owner_col == col)
            source, target = quads.at[slot, quad], final.at[col, core]
            copy = pltpu.make_async_remote_copy(
                src_ref=source,
                dst_ref=target,
                send_sem=final_send.at[slot, quad],
                recv_sem=final_recv,
                device_id={"row": owner_row, "col": owner_col},
                device_id_type=MESH,
            )

            @pl.when(here)
            def _(source=source, target=target):
                pltpu.make_async_copy(source, target, final_recv).start()

            @pl.when(jnp.logical_not(here))
            def _(copy=copy):
                copy.start()

            owners.append((here, copy))

    lax.fori_loop(0, STAGES // 2, prepare, 0)

    arrived("up", LEFT, SECOND)
    forward("up", LEFT, FAR, second_halves[low_half])
    forward("over", LEFT, ACROSS_LEFT, SECOND)
    arrived("down", RIGHT, SECOND)
    forward("down", RIGHT, FAR, second_halves[high_half])
    forward("over", RIGHT, ACROSS_RIGHT, SECOND)
    arrived("over", ACROSS, FIRST)
    forward("up", ACROSS, ACROSS_LEFT, FIRST)
    forward("down", ACROSS, ACROSS_RIGHT, FIRST)

    lax.fori_loop(STAGES // 2, STAGES, prepare, 0)

    own_copy.wait()
    multiply((OWN,), 0, TILES, False)
    to_core(OWN)

    arrived("up", LEFT, FIRST)
    forward("up", LEFT, FAR, first_halves[low_half])
    arrived("down", RIGHT, FIRST)
    forward("down", RIGHT, FAR, first_halves[high_half])
    to_z(OWN)
    multiply((LEFT, RIGHT), 0, TILES, False)
    to_core(LEFT)
    to_core(RIGHT)

    arrived("up", FAR, second_halves[low_half])
    arrived("down", FAR, second_halves[high_half])
    forward("over", FAR, ACROSS_FAR, SECOND)
    to_x(OWN)
    to_z(LEFT)
    to_z(RIGHT)

    arrived("over", ACROSS, SECOND)
    multiply((ACROSS,), 0, TILES, False)
    to_core(ACROSS)
    to_owner(OWN)
    to_x(LEFT)
    to_x(RIGHT)
    to_z(ACROSS)

    arrived("up", ACROSS_LEFT, FIRST)
    forward("up", ACROSS_LEFT, ACROSS_FAR, first_halves[low_half])
    arrived("down", ACROSS_RIGHT, FIRST)
    forward("down", ACROSS_RIGHT, ACROSS_FAR, first_halves[high_half])
    arrived("over", ACROSS_LEFT, SECOND)
    arrived("over", ACROSS_RIGHT, SECOND)
    multiply((ACROSS_LEFT, ACROSS_RIGHT), 0, TILES, False)
    to_core(ACROSS_LEFT)
    to_core(ACROSS_RIGHT)
    to_owner(LEFT)
    to_owner(RIGHT)
    to_x(ACROSS)

    arrived("up", FAR, first_halves[low_half])
    arrived("down", FAR, first_halves[high_half])
    to_z(ACROSS_LEFT)
    to_z(ACROSS_RIGHT)
    multiply((FAR,), 0, TILES, False)
    to_core(FAR)
    to_owner(ACROSS)

    arrived("over", ACROSS_FAR, SECOND)
    multiply((ACROSS_FAR,), SPLIT // TILE, TILES, False)
    to_z(FAR)
    arrived("up", ACROSS_FAR, first_halves[low_half])
    arrived("down", ACROSS_FAR, first_halves[high_half])
    multiply((ACROSS_FAR,), 0, SPLIT // TILE, True)
    to_core(ACROSS_FAR)
    to_x(ACROSS_LEFT)
    to_x(ACROSS_RIGHT)
    to_z(ACROSS_FAR)
    to_owner(ACROSS_LEFT)
    to_owner(ACROSS_RIGHT)
    to_x(FAR)
    to_owner(FAR)
    to_x(ACROSS_FAR)
    to_owner(ACROSS_FAR)

    landed(final, final_recv)
    for orbital in range(8):
        for side in range(2):
            size = min(WIDTH - side * HALF, HALF)
            for pair in range(QUAD):
                base = pair_ref[pair] - block_ref[orbital]
                below = base - virt_ref[:, pl.ds(side * HALF, size)]
                out_ref[pl.ds(pair, 1), orbital, pl.ds(side * HALF, size)] = (
                    final[orbital, side, pl.ds(pair, 1), pl.ds(0, size)] / below
                )

    for copy in sends:
        copy.wait_send()
    for slot in range(8):
        landed(z_in.at[slot], z_send.at[slot])
    for here, copy in owners:

        @pl.when(jnp.logical_not(here))
        def _(copy=copy):
            copy.wait_send()


def per_device(amplitudes, integrals, pair_energy, block_energy, virtual_energy):
    shard = jnp.transpose(amplitudes, (1, 2, 0)).reshape(DEPTH, PAIRS)
    f32, b16 = jnp.float32, jnp.bfloat16
    dma = pltpu.SemaphoreType.DMA
    return pl.pallas_call(
        kernel,
        out_shape=jax.ShapeDtypeStruct((QUAD, 8, WIDTH), f32),
        in_specs=[
            pl.BlockSpec(memory_space=pl.ANY),
            pl.BlockSpec(memory_space=pl.ANY),
            pl.BlockSpec(memory_space=pltpu.SMEM),
            pl.BlockSpec(memory_space=pltpu.SMEM),
            pl.BlockSpec(memory_space=pltpu.VMEM),
        ],
        out_specs=pl.BlockSpec(memory_space=pltpu.VMEM),
        scratch_shapes=[
            pltpu.VMEM((8, DEPTH, PAIRS), f32),
            pltpu.VMEM((SLOTS, STAGE, WIDTH), f32),
            pltpu.VMEM((TILES * TILE_PAD, PADDED), b16),
            pltpu.VMEM((TILES * TILE_PAD, PADDED), b16),
            pltpu.VMEM((4 * PAIRS, TILES * TILE_PAD), b16),
            pltpu.VMEM((8, PAIRS, PADDED), f32),
            pltpu.VMEM((8, PAIRS, HALF), f32),
            pltpu.VMEM((8, PAIRS, HALF), f32),
            pltpu.VMEM((8, Z_SIZE - 1, BLOCK, HALF), f32),
            pltpu.VMEM((8, BLOCK, HALF), f32),
            pltpu.VMEM((8, PART, HALF), f32),
            pltpu.VMEM((8, 2, QUAD, HALF), f32),
            pltpu.VMEM((8, 2, QUAD, HALF), f32),
            dma,
            dma((SLOTS,)),
            dma((6,)),
            dma((6,)),
            dma((6,)),
            dma((6,)),
            dma((5,)),
            dma((5,)),
            dma((8,)),
            dma((8,)),
            dma((8,)),
            dma((8,)),
            dma((8,)),
            dma((8,)),
            dma((8, 2)),
            dma,
        ],
        compiler_params=pltpu.CompilerParams(
            collective_id=0, has_side_effects=True, vmem_limit_bytes=62 * 1024 * 1024
        ),
    )(shard, integrals, pair_energy, block_energy, virtual_energy.reshape(1, WIDTH))


def solution(mesh):
    placed = (P("col", "row", None), P("row", None, "col", None), P(("row", "col")), P(), P())
    return jax.shard_map(
        per_device,
        mesh=mesh,
        in_specs=placed,
        out_specs=P(("row", "col"), None, None),
        check_vma=False,
    )
```

```python
import functools

import jax
import jax.numpy as jnp
from jax import lax
from jax.experimental import pallas as pl
from jax.experimental.pallas import tpu as pltpu
from jax.sharding import PartitionSpec as P

MESH = pl.DeviceIdType.MESH

OWN, LEFT, RIGHT, ACROSS, ACROSS_LEFT, ACROSS_RIGHT, FAR, ACROSS_FAR = range(8)
Y_SIZE, Z_SIZE = 4, 8
PAIRS = 128
WIDTH = 1200
PADDED = 1280
HALF = PADDED // 2
DEPTH = 2400
TILE = 480
TILES = DEPTH // TILE
TILE_PAD = 512
STAGE = 240
STAGES = DEPTH // STAGE
SLOTS = 4
SPLIT = 3 * TILE
FIRST = (0, SPLIT)
SECOND = (SPLIT, DEPTH - SPLIT)
BLOCK = PAIRS // Z_SIZE
PART = BLOCK // 2
QUAD = 4
LONG, SHORT = 0, 1
HOPS = (4, 3)
COLUMN = 256


def halves(rows):
    start, size = rows
    return (start, size // 2), (start + size // 2, size // 2)


def kernel(
    amp_ref,
    int_ref,
    pair_ref,
    block_ref,
    virt_ref,
    out_ref,
    gathered,
    stage,
    b_high,
    b_low,
    lhs,
    partial,
    core_in,
    summed,
    z_in,
    z_sum,
    x_in,
    quads,
    final,
    own_sem,
    stage_sem,
    up_send,
    up_recv,
    down_send,
    down_recv,
    over_send,
    over_recv,
    core_send,
    core_recv,
    z_send,
    z_recv,
    x_send,
    x_recv,
    final_send,
    final_recv,
):
    row = lax.axis_index("row")
    col = lax.axis_index("col")
    x_hi, z, core = row // 16, (row // 2) % Z_SIZE, row % 2
    x_lo, y = col // Y_SIZE, col % Y_SIZE

    up = {"row": row, "col": x_lo * Y_SIZE + (y + 1) % Y_SIZE}
    down = {"row": row, "col": x_lo * Y_SIZE + (y + 3) % Y_SIZE}
    over = {"row": row, "col": (1 - x_lo) * Y_SIZE + y}
    partner = {"row": row + 1 - 2 * core, "col": col}
    opposite = {"row": row + 16 - 32 * x_hi, "col": col}

    def at_z(step):
        return {"row": x_hi * 16 + ((z + step) % Z_SIZE) * 2 + core, "col": col}

    def load(index):
        slot = index % SLOTS
        source = int_ref.at[index // 5, pl.ds((index % 5) * STAGE, STAGE), 0]
        return pltpu.make_async_copy(source, stage.at[slot], stage_sem.at[slot])

    own_copy = pltpu.make_async_copy(amp_ref, gathered.at[OWN], own_sem)
    for index in range(SLOTS):
        load(index).start()

    barrier = pltpu.get_barrier_semaphore()

    def greet(device):
        pl.semaphore_signal(barrier, inc=1, device_id=device, device_id_type=MESH)

    for device in (up, down, over, partner, opposite):
        greet(device)
    for step in (1, Z_SIZE - 1):
        greet(at_z(step))
    source_z = 2 * (row % 4) + col // 4
    source_row = ((col % 4) // 2) * 16 + source_z * 2
    for other_col in range(8):
        for other_core in range(2):
            greet({"row": source_row + other_core, "col": other_col})
    own_copy.start()
    pl.semaphore_wait(barrier, 5 + 2 + 16)

    sends = []

    def send(source, target, send_sem, recv_sem, device):
        copy = pltpu.make_async_remote_copy(
            src_ref=source,
            dst_ref=target,
            send_sem=send_sem,
            recv_sem=recv_sem,
            device_id=device,
            device_id_type=MESH,
        )
        copy.start()
        return copy

    def landed(ref, sem):
        pltpu.make_async_copy(ref, ref, sem).wait()

    counts = {"up": 0, "down": 0, "over": 0}
    lanes = {
        "up": (up, up_send, up_recv),
        "down": (down, down_send, down_recv),
        "over": (over, over_send, over_recv),
    }
    arrivals = {}

    def forward(lane, source, target, rows):
        device, send_sem, recv_sem = lanes[lane]
        index = counts[lane]
        counts[lane] = index + 1
        start, size = rows
        if source == OWN:
            source_ref = amp_ref.at[pl.ds(start, size)]
        else:
            source_ref = gathered.at[source, pl.ds(start, size)]
        target_ref = gathered.at[target, pl.ds(start, size)]
        sends.append(send(source_ref, target_ref, send_sem.at[index], recv_sem.at[index], device))
        arrivals[(lane, target, rows)] = (target_ref, recv_sem.at[index])

    def arrived(lane, target, rows):
        landed(*arrivals.pop((lane, target, rows)))

    low_half, high_half = range(2)
    second_halves, first_halves = halves(SECOND), halves(FIRST)

    forward("up", OWN, LEFT, SECOND)
    forward("down", OWN, RIGHT, SECOND)
    forward("over", OWN, ACROSS, FIRST)
    forward("up", OWN, LEFT, FIRST)
    forward("down", OWN, RIGHT, FIRST)
    forward("over", OWN, ACROSS, SECOND)

    for tile in range(TILES):
        zeros = jnp.zeros((TILE_PAD - TILE, PADDED), jnp.bfloat16)
        b_high[pl.ds(tile * TILE_PAD + TILE, TILE_PAD - TILE), :] = zeros
        b_low[pl.ds(tile * TILE_PAD + TILE, TILE_PAD - TILE), :] = zeros

    def prepare(index, carry):
        load(index).wait()
        value = stage[index % SLOTS]
        high = value.astype(jnp.bfloat16)
        low = (value - high.astype(jnp.float32)).astype(jnp.bfloat16)
        start = pl.multiple_of((index // 2) * TILE_PAD + (index % 2) * STAGE, 16)
        b_high[pl.ds(start, STAGE), pl.ds(0, WIDTH)] = high
        b_low[pl.ds(start, STAGE), pl.ds(0, WIDTH)] = low

        @pl.when(index + SLOTS < STAGES)
        def _():
            load(index + SLOTS).start()

        return carry

    def split(slot, place, places, first, last):
        def body(tile, carry):
            value = gathered[slot, pl.ds(pl.multiple_of(tile * TILE, 8), TILE), :]
            value = jnp.concatenate([value, jnp.zeros((TILE_PAD - TILE, PAIRS), jnp.float32)], axis=0).T
            high = value.astype(jnp.bfloat16)
            low = (value - high.astype(jnp.float32)).astype(jnp.bfloat16)
            lanes_of = pl.ds(pl.multiple_of(tile * TILE_PAD, TILE_PAD), TILE_PAD)
            lhs[pl.ds(place * PAIRS, PAIRS), lanes_of] = high
            lhs[pl.ds((places + place) * PAIRS, PAIRS), lanes_of] = low
            return carry

        lax.fori_loop(first, last, body, 0)

    def multiply(slots, first, last, add):
        places = len(slots)
        rows = places * PAIRS
        for place, slot in enumerate(slots):
            split(slot, place, places, first, last)
        depth = pl.ds(first * TILE_PAD, (last - first) * TILE_PAD)

        def body(step, carry):
            columns = pl.ds(pl.multiple_of(step * COLUMN, COLUMN), COLUMN)
            both = jnp.dot(lhs[pl.ds(0, 2 * rows), depth], b_high[depth, columns], preferred_element_type=jnp.float32)
            rest = jnp.dot(lhs[pl.ds(0, rows), depth], b_low[depth, columns], preferred_element_type=jnp.float32)
            total = both[:rows] + (both[rows:] + rest)
            for place, slot in enumerate(slots):
                piece = total[place * PAIRS : (place + 1) * PAIRS]
                if add:
                    piece = piece + partial[slot, :, columns]
                partial[slot, :, columns] = piece
            return carry

        lax.fori_loop(0, PADDED // COLUMN, body, 0)

    kept = pl.ds(pl.multiple_of(core * HALF, 128), HALF)
    given = pl.ds(pl.multiple_of((1 - core) * HALF, 128), HALF)

    def to_core(slot):
        sends.append(
            send(partial.at[slot, :, given], core_in.at[slot], core_send.at[slot], core_recv.at[slot], partner)
        )

    def to_z(slot):
        landed(core_in.at[slot], core_recv.at[slot])
        summed[slot] = partial[slot, :, kept] + core_in[slot]
        along(slot, LONG, 0)
        along(slot, SHORT, 0)

    def block_at(step):
        return pl.ds(pl.multiple_of(((z + step) % Z_SIZE) * BLOCK, BLOCK), BLOCK)

    def along(slot, chain, hop):
        way = (1 if slot % 2 == 0 else -1) * (1 if chain == LONG else -1)
        block = block_at(way * (HOPS[chain] - hop) + Z_SIZE)
        place = chain * HOPS[LONG] + hop
        if hop:
            came = z_in.at[slot, place - 1]
            landed(came, z_recv.at[slot, place - 1])
            summed[slot, block] = summed[slot, block] + came[...]
        send(
            summed.at[slot, block],
            z_in.at[slot, place],
            z_send.at[slot],
            z_recv.at[slot, place],
            at_z(way + Z_SIZE),
        )

    def z_step(slot, hop):
        along(slot, LONG, hop)
        if hop < HOPS[SHORT]:
            along(slot, SHORT, hop)

    def to_x(slot):
        total = summed[slot, block_at(0)]
        for chain in (SHORT, LONG):
            place = chain * HOPS[LONG] + HOPS[chain] - 1
            landed(z_in.at[slot, place], z_recv.at[slot, place])
            total = total + z_in[slot, place]
        z_sum[slot] = total
        start = pl.multiple_of((1 - x_hi) * PART, PART)
        sends.append(
            send(z_sum.at[slot, pl.ds(start, PART)], x_in.at[slot], x_send.at[slot], x_recv.at[slot], opposite)
        )

    def chunk_col(slot):
        shift = {OWN: 0, LEFT: 3, RIGHT: 1, ACROSS: 0, ACROSS_LEFT: 3, ACROSS_RIGHT: 1, FAR: 2, ACROSS_FAR: 2}[slot]
        side = x_lo if slot in (OWN, LEFT, RIGHT, FAR) else 1 - x_lo
        return side * Y_SIZE + (y + shift) % Y_SIZE

    owners = []

    def to_owner(slot):
        landed(x_in.at[slot], x_recv.at[slot])
        total = z_sum[slot, pl.ds(pl.multiple_of(x_hi * PART, PART), PART), :] + x_in[slot]
        owner_row = 4 * chunk_col(slot) + z // 2
        for quad in range(2):
            quads[slot, quad] = total[quad * QUAD : (quad + 1) * QUAD]
            owner_col = 4 * (z % 2) + 2 * x_hi + quad
            here = jnp.logical_and(owner_row == row, owner_col == col)
            source, target = quads.at[slot, quad], final.at[col, core]
            copy = pltpu.make_async_remote_copy(
                src_ref=source,
                dst_ref=target,
                send_sem=final_send.at[slot, quad],
                recv_sem=final_recv,
                device_id={"row": owner_row, "col": owner_col},
                device_id_type=MESH,
            )

            @pl.when(here)
            def _(source=source, target=target):
                pltpu.make_async_copy(source, target, final_recv).start()

            @pl.when(jnp.logical_not(here))
            def _(copy=copy):
                copy.start()

            owners.append((here, copy))

    active = []

    def reduce(*slots):
        for slot in slots:
            to_core(slot)
            active.append([slot, 0])

    def pump():
        for entry in list(active):
            slot, stage_of = entry
            if stage_of == 0:
                to_z(slot)
            elif stage_of < HOPS[LONG]:
                z_step(slot, stage_of)
            elif stage_of == HOPS[LONG]:
                to_x(slot)
            else:
                to_owner(slot)
                active.remove(entry)
            entry[1] = stage_of + 1

    lax.fori_loop(0, STAGES // 2, prepare, 0)

    arrived("up", LEFT, SECOND)
    forward("up", LEFT, FAR, second_halves[low_half])
    forward("over", LEFT, ACROSS_LEFT, SECOND)
    arrived("down", RIGHT, SECOND)
    forward("down", RIGHT, FAR, second_halves[high_half])
    forward("over", RIGHT, ACROSS_RIGHT, SECOND)
    arrived("over", ACROSS, FIRST)
    forward("up", ACROSS, ACROSS_LEFT, FIRST)
    forward("down", ACROSS, ACROSS_RIGHT, FIRST)

    lax.fori_loop(STAGES // 2, STAGES, prepare, 0)

    own_copy.wait()
    multiply((OWN,), 0, TILES, False)
    reduce(OWN)

    arrived("up", LEFT, FIRST)
    forward("up", LEFT, FAR, first_halves[low_half])
    arrived("down", RIGHT, FIRST)
    forward("down", RIGHT, FAR, first_halves[high_half])
    pump()
    multiply((LEFT, RIGHT), 0, TILES, False)
    reduce(LEFT, RIGHT)
    pump()

    arrived("up", FAR, second_halves[low_half])
    arrived("down", FAR, second_halves[high_half])
    forward("over", FAR, ACROSS_FAR, SECOND)
    arrived("over", ACROSS, SECOND)
    multiply((ACROSS,), 0, TILES, False)
    reduce(ACROSS)
    pump()
    pump()
    pump()

    arrived("up", ACROSS_LEFT, FIRST)
    forward("up", ACROSS_LEFT, ACROSS_FAR, first_halves[low_half])
    arrived("down", ACROSS_RIGHT, FIRST)
    forward("down", ACROSS_RIGHT, ACROSS_FAR, first_halves[high_half])
    pump()
    arrived("over", ACROSS_LEFT, SECOND)
    arrived("over", ACROSS_RIGHT, SECOND)
    multiply((ACROSS_LEFT, ACROSS_RIGHT), 0, TILES, False)
    reduce(ACROSS_LEFT, ACROSS_RIGHT)
    pump()

    arrived("up", FAR, first_halves[low_half])
    arrived("down", FAR, first_halves[high_half])
    pump()
    multiply((FAR,), 0, TILES, False)
    reduce(FAR)
    pump()

    arrived("over", ACROSS_FAR, SECOND)
    multiply((ACROSS_FAR,), SPLIT // TILE, TILES, False)
    pump()
    arrived("up", ACROSS_FAR, first_halves[low_half])
    arrived("down", ACROSS_FAR, first_halves[high_half])
    multiply((ACROSS_FAR,), 0, SPLIT // TILE, True)
    reduce(ACROSS_FAR)
    while active:
        pump()

    landed(final, final_recv)
    for orbital in range(8):
        for side in range(2):
            size = min(WIDTH - side * HALF, HALF)
            for pair in range(QUAD):
                base = pair_ref[pair] - block_ref[orbital]
                below = base - virt_ref[:, pl.ds(side * HALF, size)]
                out_ref[pl.ds(pair, 1), orbital, pl.ds(side * HALF, size)] = (
                    final[orbital, side, pl.ds(pair, 1), pl.ds(0, size)] / below
                )

    for copy in sends:
        copy.wait_send()
    for slot in range(8):
        landed(z_in.at[slot], z_send.at[slot])
    for here, copy in owners:

        @pl.when(jnp.logical_not(here))
        def _(copy=copy):
            copy.wait_send()


def per_device(amplitudes, integrals, pair_energy, block_energy, virtual_energy):
    shard = jnp.transpose(amplitudes, (1, 2, 0)).reshape(DEPTH, PAIRS)
    f32, b16 = jnp.float32, jnp.bfloat16
    dma = pltpu.SemaphoreType.DMA
    return pl.pallas_call(
        kernel,
        out_shape=jax.ShapeDtypeStruct((QUAD, 8, WIDTH), f32),
        in_specs=[
            pl.BlockSpec(memory_space=pl.ANY),
            pl.BlockSpec(memory_space=pl.ANY),
            pl.BlockSpec(memory_space=pltpu.SMEM),
            pl.BlockSpec(memory_space=pltpu.SMEM),
            pl.BlockSpec(memory_space=pltpu.VMEM),
        ],
        out_specs=pl.BlockSpec(memory_space=pltpu.VMEM),
        scratch_shapes=[
            pltpu.VMEM((8, DEPTH, PAIRS), f32),
            pltpu.VMEM((SLOTS, STAGE, WIDTH), f32),
            pltpu.VMEM((TILES * TILE_PAD, PADDED), b16),
            pltpu.VMEM((TILES * TILE_PAD, PADDED), b16),
            pltpu.VMEM((4 * PAIRS, TILES * TILE_PAD), b16),
            pltpu.VMEM((8, PAIRS, PADDED), f32),
            pltpu.VMEM((8, PAIRS, HALF), f32),
            pltpu.VMEM((8, PAIRS, HALF), f32),
            pltpu.VMEM((8, Z_SIZE - 1, BLOCK, HALF), f32),
            pltpu.VMEM((8, BLOCK, HALF), f32),
            pltpu.VMEM((8, PART, HALF), f32),
            pltpu.VMEM((8, 2, QUAD, HALF), f32),
            pltpu.VMEM((8, 2, QUAD, HALF), f32),
            dma,
            dma((SLOTS,)),
            dma((6,)),
            dma((6,)),
            dma((6,)),
            dma((6,)),
            dma((5,)),
            dma((5,)),
            dma((8,)),
            dma((8,)),
            dma((8,)),
            dma((8, Z_SIZE - 1)),
            dma((8,)),
            dma((8,)),
            dma((8, 2)),
            dma,
        ],
        compiler_params=pltpu.CompilerParams(
            collective_id=0, has_side_effects=True, vmem_limit_bytes=62 * 1024 * 1024
        ),
    )(shard, integrals, pair_energy, block_energy, virtual_energy.reshape(1, WIDTH))


def solution(mesh):
    placed = (P("col", "row", None), P("row", None, "col", None), P(("row", "col")), P(), P())
    return jax.shard_map(
        per_device,
        mesh=mesh,
        in_specs=placed,
        out_specs=P(("row", "col"), None, None),
        check_vma=False,
    )
```

```python
import functools

import jax
import jax.numpy as jnp
from jax import lax
from jax.experimental import pallas as pl
from jax.experimental.pallas import tpu as pltpu
from jax.sharding import PartitionSpec as P

MESH = pl.DeviceIdType.MESH

OWN, LEFT, RIGHT, ACROSS, ACROSS_LEFT, ACROSS_RIGHT, FAR, ACROSS_FAR = range(8)
Y_SIZE, Z_SIZE = 4, 8
PAIRS = 128
WIDTH = 1200
PADDED = 1280
HALF = PADDED // 2
DEPTH = 2400
TILE = 480
TILES = DEPTH // TILE
TILE_PAD = 512
STAGE = 240
STAGES = DEPTH // STAGE
SLOTS = 4
SPLIT = 3 * TILE
FIRST = (0, SPLIT)
SECOND = (SPLIT, DEPTH - SPLIT)
BLOCK = PAIRS // Z_SIZE
PART = BLOCK // 2
QUAD = 4
LONG, SHORT = 0, 1
HOPS = (4, 3)
COLUMN = 256


def halves(rows):
    start, size = rows
    return (start, size // 2), (start + size // 2, size // 2)


def kernel(
    amp_ref,
    int_ref,
    pair_ref,
    block_ref,
    virt_ref,
    out_ref,
    gathered,
    stage,
    b_high,
    b_low,
    lhs,
    partial,
    core_in,
    summed,
    z_in,
    z_sum,
    x_in,
    quads,
    final,
    own_sem,
    stage_sem,
    up_send,
    up_recv,
    down_send,
    down_recv,
    over_send,
    over_recv,
    core_send,
    core_recv,
    z_send,
    z_recv,
    x_send,
    x_recv,
    final_send,
    final_recv,
):
    row = lax.axis_index("row")
    col = lax.axis_index("col")
    x_hi, z, core = row // 16, (row // 2) % Z_SIZE, row % 2
    x_lo, y = col // Y_SIZE, col % Y_SIZE

    up = {"row": row, "col": x_lo * Y_SIZE + (y + 1) % Y_SIZE}
    down = {"row": row, "col": x_lo * Y_SIZE + (y + 3) % Y_SIZE}
    over = {"row": row, "col": (1 - x_lo) * Y_SIZE + y}
    partner = {"row": row + 1 - 2 * core, "col": col}
    opposite = {"row": row + 16 - 32 * x_hi, "col": col}

    def at_z(step):
        return {"row": x_hi * 16 + ((z + step) % Z_SIZE) * 2 + core, "col": col}

    def load(index):
        slot = index % SLOTS
        source = int_ref.at[index // 5, pl.ds((index % 5) * STAGE, STAGE), 0]
        return pltpu.make_async_copy(source, stage.at[slot], stage_sem.at[slot])

    own_copy = pltpu.make_async_copy(amp_ref, gathered.at[OWN], own_sem)
    for index in range(SLOTS):
        load(index).start()

    barrier = pltpu.get_barrier_semaphore()

    def greet(device):
        pl.semaphore_signal(barrier, inc=1, device_id=device, device_id_type=MESH)

    for device in (up, down, over, partner, opposite):
        greet(device)
    for step in (1, Z_SIZE - 1):
        greet(at_z(step))
    source_z = 2 * (row % 4) + col // 4
    source_row = ((col % 4) // 2) * 16 + source_z * 2
    for other_col in range(8):
        for other_core in range(2):
            greet({"row": source_row + other_core, "col": other_col})
    own_copy.start()
    pl.semaphore_wait(barrier, 5 + 2 + 16)

    sends = []

    def send(source, target, send_sem, recv_sem, device):
        copy = pltpu.make_async_remote_copy(
            src_ref=source,
            dst_ref=target,
            send_sem=send_sem,
            recv_sem=recv_sem,
            device_id=device,
            device_id_type=MESH,
        )
        copy.start()
        return copy

    def landed(ref, sem):
        pltpu.make_async_copy(ref, ref, sem).wait()

    counts = {"up": 0, "down": 0, "over": 0}
    lanes = {
        "up": (up, up_send, up_recv),
        "down": (down, down_send, down_recv),
        "over": (over, over_send, over_recv),
    }
    arrivals = {}

    def forward(lane, source, target, rows):
        device, send_sem, recv_sem = lanes[lane]
        index = counts[lane]
        counts[lane] = index + 1
        start, size = rows
        if source == OWN:
            source_ref = amp_ref.at[pl.ds(start, size)]
        else:
            source_ref = gathered.at[source, pl.ds(start, size)]
        target_ref = gathered.at[target, pl.ds(start, size)]
        sends.append(send(source_ref, target_ref, send_sem.at[index], recv_sem.at[index], device))
        arrivals[(lane, target, rows)] = (target_ref, recv_sem.at[index])

    def arrived(lane, target, rows):
        landed(*arrivals.pop((lane, target, rows)))

    low_half, high_half = range(2)
    second_halves, first_halves = halves(SECOND), halves(FIRST)

    forward("up", OWN, LEFT, SECOND)
    forward("down", OWN, RIGHT, SECOND)
    forward("over", OWN, ACROSS, FIRST)
    forward("up", OWN, LEFT, FIRST)
    forward("down", OWN, RIGHT, FIRST)
    forward("over", OWN, ACROSS, SECOND)

    for tile in range(TILES):
        zeros = jnp.zeros((TILE_PAD - TILE, PADDED), jnp.bfloat16)
        b_high[pl.ds(tile * TILE_PAD + TILE, TILE_PAD - TILE), :] = zeros
        b_low[pl.ds(tile * TILE_PAD + TILE, TILE_PAD - TILE), :] = zeros

    def prepare(index, carry):
        load(index).wait()
        value = stage[index % SLOTS]
        high = value.astype(jnp.bfloat16)
        low = (value - high.astype(jnp.float32)).astype(jnp.bfloat16)
        start = pl.multiple_of((index // 2) * TILE_PAD + (index % 2) * STAGE, 16)
        b_high[pl.ds(start, STAGE), pl.ds(0, WIDTH)] = high
        b_low[pl.ds(start, STAGE), pl.ds(0, WIDTH)] = low

        @pl.when(index + SLOTS < STAGES)
        def _():
            load(index + SLOTS).start()

        return carry

    def split(slot, place, places, first, last):
        def body(tile, carry):
            value = gathered[slot, pl.ds(pl.multiple_of(tile * TILE, 8), TILE), :]
            value = jnp.concatenate([value, jnp.zeros((TILE_PAD - TILE, PAIRS), jnp.float32)], axis=0).T
            high = value.astype(jnp.bfloat16)
            low = (value - high.astype(jnp.float32)).astype(jnp.bfloat16)
            lanes_of = pl.ds(pl.multiple_of(tile * TILE_PAD, TILE_PAD), TILE_PAD)
            lhs[pl.ds(place * PAIRS, PAIRS), lanes_of] = high
            lhs[pl.ds((places + place) * PAIRS, PAIRS), lanes_of] = low
            return carry

        lax.fori_loop(first, last, body, 0)

    def multiply(slots, first, last, add):
        places = len(slots)
        rows = places * PAIRS
        for place, slot in enumerate(slots):
            split(slot, place, places, first, last)
        depth = pl.ds(first * TILE_PAD, (last - first) * TILE_PAD)

        def body(step, carry):
            columns = pl.ds(pl.multiple_of(step * COLUMN, COLUMN), COLUMN)
            both = jnp.dot(lhs[pl.ds(0, 2 * rows), depth], b_high[depth, columns], preferred_element_type=jnp.float32)
            rest = jnp.dot(lhs[pl.ds(0, rows), depth], b_low[depth, columns], preferred_element_type=jnp.float32)
            total = both[:rows] + (both[rows:] + rest)
            for place, slot in enumerate(slots):
                piece = total[place * PAIRS : (place + 1) * PAIRS]
                if add:
                    piece = piece + partial[slot, :, columns]
                partial[slot, :, columns] = piece
            return carry

        lax.fori_loop(0, PADDED // COLUMN, body, 0)

    kept = pl.ds(pl.multiple_of(core * HALF, 128), HALF)
    given = pl.ds(pl.multiple_of((1 - core) * HALF, 128), HALF)

    def to_core(slot):
        sends.append(
            send(partial.at[slot, :, given], core_in.at[slot], core_send.at[slot], core_recv.at[slot], partner)
        )

    def to_z(slot):
        landed(core_in.at[slot], core_recv.at[slot])
        summed[slot] = partial[slot, :, kept] + core_in[slot]
        along(slot, LONG, 0)
        along(slot, SHORT, 0)

    def block_at(step):
        return pl.ds(pl.multiple_of(((z + step) % Z_SIZE) * BLOCK, BLOCK), BLOCK)

    def along(slot, chain, hop):
        way = (1 if slot % 2 == 0 else -1) * (1 if chain == LONG else -1)
        block = block_at(way * (HOPS[chain] - hop) + Z_SIZE)
        place = chain * HOPS[LONG] + hop
        if hop:
            came = z_in.at[slot, place - 1]
            landed(came, z_recv.at[slot, place - 1])
            summed[slot, block] = summed[slot, block] + came[...]
        send(
            summed.at[slot, block],
            z_in.at[slot, place],
            z_send.at[slot],
            z_recv.at[slot, place],
            at_z(way + Z_SIZE),
        )

    def z_step(slot, hop):
        along(slot, LONG, hop)
        if hop < HOPS[SHORT]:
            along(slot, SHORT, hop)

    def to_x(slot):
        total = summed[slot, block_at(0)]
        for chain in (SHORT, LONG):
            place = chain * HOPS[LONG] + HOPS[chain] - 1
            landed(z_in.at[slot, place], z_recv.at[slot, place])
            total = total + z_in[slot, place]
        z_sum[slot] = total
        start = pl.multiple_of((1 - x_hi) * PART, PART)
        sends.append(
            send(z_sum.at[slot, pl.ds(start, PART)], x_in.at[slot], x_send.at[slot], x_recv.at[slot], opposite)
        )

    def chunk_col(slot):
        shift = {OWN: 0, LEFT: 3, RIGHT: 1, ACROSS: 0, ACROSS_LEFT: 3, ACROSS_RIGHT: 1, FAR: 2, ACROSS_FAR: 2}[slot]
        side = x_lo if slot in (OWN, LEFT, RIGHT, FAR) else 1 - x_lo
        return side * Y_SIZE + (y + shift) % Y_SIZE

    owners = []

    def to_owner(slot):
        landed(x_in.at[slot], x_recv.at[slot])
        total = z_sum[slot, pl.ds(pl.multiple_of(x_hi * PART, PART), PART), :] + x_in[slot]
        owner_row = 4 * chunk_col(slot) + z // 2
        for quad in range(2):
            quads[slot, quad] = total[quad * QUAD : (quad + 1) * QUAD]
            owner_col = 4 * (z % 2) + 2 * x_hi + quad
            here = jnp.logical_and(owner_row == row, owner_col == col)
            source, target = quads.at[slot, quad], final.at[col, core]
            copy = pltpu.make_async_remote_copy(
                src_ref=source,
                dst_ref=target,
                send_sem=final_send.at[slot, quad],
                recv_sem=final_recv,
                device_id={"row": owner_row, "col": owner_col},
                device_id_type=MESH,
            )

            @pl.when(here)
            def _(source=source, target=target):
                pltpu.make_async_copy(source, target, final_recv).start()

            @pl.when(jnp.logical_not(here))
            def _(copy=copy):
                copy.start()

            owners.append((here, copy))

    active = []

    def reduce(*slots):
        for slot in slots:
            to_core(slot)
            active.append([slot, 0])

    def pump(last=False):
        for entry in list(active):
            slot, stage_of = entry
            if stage_of > HOPS[LONG] and not last:
                continue
            if stage_of == 0:
                to_z(slot)
            elif stage_of < HOPS[LONG]:
                z_step(slot, stage_of)
            elif stage_of == HOPS[LONG]:
                to_x(slot)
            else:
                to_owner(slot)
                active.remove(entry)
            entry[1] = stage_of + 1

    lax.fori_loop(0, STAGES // 2, prepare, 0)

    arrived("up", LEFT, SECOND)
    forward("up", LEFT, FAR, second_halves[low_half])
    forward("over", LEFT, ACROSS_LEFT, SECOND)
    arrived("down", RIGHT, SECOND)
    forward("down", RIGHT, FAR, second_halves[high_half])
    forward("over", RIGHT, ACROSS_RIGHT, SECOND)
    arrived("over", ACROSS, FIRST)
    forward("up", ACROSS, ACROSS_LEFT, FIRST)
    forward("down", ACROSS, ACROSS_RIGHT, FIRST)

    lax.fori_loop(STAGES // 2, STAGES, prepare, 0)

    own_copy.wait()
    multiply((OWN,), 0, TILES, False)
    reduce(OWN)

    arrived("up", LEFT, FIRST)
    forward("up", LEFT, FAR, first_halves[low_half])
    arrived("down", RIGHT, FIRST)
    forward("down", RIGHT, FAR, first_halves[high_half])
    pump()
    multiply((LEFT, RIGHT), 0, TILES, False)
    reduce(LEFT, RIGHT)
    pump()

    arrived("up", FAR, second_halves[low_half])
    arrived("down", FAR, second_halves[high_half])
    forward("over", FAR, ACROSS_FAR, SECOND)
    arrived("over", ACROSS, SECOND)
    multiply((ACROSS,), 0, TILES, False)
    reduce(ACROSS)
    pump()
    pump()
    pump()

    arrived("up", ACROSS_LEFT, FIRST)
    forward("up", ACROSS_LEFT, ACROSS_FAR, first_halves[low_half])
    arrived("down", ACROSS_RIGHT, FIRST)
    forward("down", ACROSS_RIGHT, ACROSS_FAR, first_halves[high_half])
    pump()
    arrived("over", ACROSS_LEFT, SECOND)
    arrived("over", ACROSS_RIGHT, SECOND)
    multiply((ACROSS_LEFT, ACROSS_RIGHT), 0, TILES, False)
    reduce(ACROSS_LEFT, ACROSS_RIGHT)
    pump()

    arrived("up", FAR, first_halves[low_half])
    arrived("down", FAR, first_halves[high_half])
    pump()
    multiply((FAR,), 0, TILES, False)
    reduce(FAR)
    pump()

    arrived("over", ACROSS_FAR, SECOND)
    multiply((ACROSS_FAR,), SPLIT // TILE, TILES, False)
    pump()
    arrived("up", ACROSS_FAR, first_halves[low_half])
    arrived("down", ACROSS_FAR, first_halves[high_half])
    multiply((ACROSS_FAR,), 0, SPLIT // TILE, True)
    reduce(ACROSS_FAR)
    while active:
        pump(True)

    landed(final, final_recv)
    for orbital in range(8):
        for side in range(2):
            size = min(WIDTH - side * HALF, HALF)
            for pair in range(QUAD):
                base = pair_ref[pair] - block_ref[orbital]
                below = base - virt_ref[:, pl.ds(side * HALF, size)]
                out_ref[pl.ds(pair, 1), orbital, pl.ds(side * HALF, size)] = (
                    final[orbital, side, pl.ds(pair, 1), pl.ds(0, size)] / below
                )

    for copy in sends:
        copy.wait_send()
    for slot in range(8):
        landed(z_in.at[slot], z_send.at[slot])
    for here, copy in owners:

        @pl.when(jnp.logical_not(here))
        def _(copy=copy):
            copy.wait_send()


def per_device(amplitudes, integrals, pair_energy, block_energy, virtual_energy):
    shard = jnp.transpose(amplitudes, (1, 2, 0)).reshape(DEPTH, PAIRS)
    f32, b16 = jnp.float32, jnp.bfloat16
    dma = pltpu.SemaphoreType.DMA
    return pl.pallas_call(
        kernel,
        out_shape=jax.ShapeDtypeStruct((QUAD, 8, WIDTH), f32),
        in_specs=[
            pl.BlockSpec(memory_space=pl.ANY),
            pl.BlockSpec(memory_space=pl.ANY),
            pl.BlockSpec(memory_space=pltpu.SMEM),
            pl.BlockSpec(memory_space=pltpu.SMEM),
            pl.BlockSpec(memory_space=pltpu.VMEM),
        ],
        out_specs=pl.BlockSpec(memory_space=pltpu.VMEM),
        scratch_shapes=[
            pltpu.VMEM((8, DEPTH, PAIRS), f32),
            pltpu.VMEM((SLOTS, STAGE, WIDTH), f32),
            pltpu.VMEM((TILES * TILE_PAD, PADDED), b16),
            pltpu.VMEM((TILES * TILE_PAD, PADDED), b16),
            pltpu.VMEM((4 * PAIRS, TILES * TILE_PAD), b16),
            pltpu.VMEM((8, PAIRS, PADDED), f32),
            pltpu.VMEM((8, PAIRS, HALF), f32),
            pltpu.VMEM((8, PAIRS, HALF), f32),
            pltpu.VMEM((8, Z_SIZE - 1, BLOCK, HALF), f32),
            pltpu.VMEM((8, BLOCK, HALF), f32),
            pltpu.VMEM((8, PART, HALF), f32),
            pltpu.VMEM((8, 2, QUAD, HALF), f32),
            pltpu.VMEM((8, 2, QUAD, HALF), f32),
            dma,
            dma((SLOTS,)),
            dma((6,)),
            dma((6,)),
            dma((6,)),
            dma((6,)),
            dma((5,)),
            dma((5,)),
            dma((8,)),
            dma((8,)),
            dma((8,)),
            dma((8, Z_SIZE - 1)),
            dma((8,)),
            dma((8,)),
            dma((8, 2)),
            dma,
        ],
        compiler_params=pltpu.CompilerParams(
            collective_id=0, has_side_effects=True, vmem_limit_bytes=62 * 1024 * 1024
        ),
    )(shard, integrals, pair_energy, block_energy, virtual_energy.reshape(1, WIDTH))


def solution(mesh):
    placed = (P("col", "row", None), P("row", None, "col", None), P(("row", "col")), P(), P())
    return jax.shard_map(
        per_device,
        mesh=mesh,
        in_specs=placed,
        out_specs=P(("row", "col"), None, None),
        check_vma=False,
    )
```
